32 devices in a mesh: blk: 4 (over y, x), team: 4 (over z), dp: 2 (over core).
Axes of the slice: x: 2, y: 2, z: 4, core: 2. Of those that a mesh axis runs over, the one named last changes fastest.
Arguments:
- hidden: bfloat16 [1024, 28672], P(('blk', 'dp'), 'team'), may hold values from -6 to 6
- out_grad: bfloat16 [1024, 8192], P(('blk', 'dp'), 'team'), may hold values from -0.1875 to 0.1875
- act_rows: int32 [4, 64, 12], P('team'), may hold values from 0 to 55, as said below
- col_owner: int32 [64], replicated, may hold values from 0 to 3, as said below
Outputs:
- gradients: float32 [4, 4, 288, 128, 128], P('team', 'blk', 'dp')
- scores: float32 [4, 4, 288], P('team', 'blk', 'dp')
The draws below stay inside these ranges and needn't reach their ends.
Inputs may be any that keep to these rules, and one draw needn't show every extreme that they name: For each t and c the 12 entries act_rows[t, c, :] are distinct. `col_owner`: some owner holds exactly 24 block columns and no owner holds more.
All inputs are finite; a program needn't handle non-finite values.
Results may differ from the reference program's by a relative error of at most 0.0003.
Values may be sent and summed in bfloat16 or wider, within the bound.
A program may use at most 192 MiB of HBM per device.

```python
import jax
import jax.numpy as jnp
from jax import lax

D = 8192
FF = 28672
BS = 128
KC = 12
DB = 64
FBT = 56
CAPC = 24
CAP = 288
TOKENS = 1024
N_BLK = 4
N_TEAM = 4


def draw_act_rows(key, part):
    key_list = jax.random.split(key, N_TEAM * DB)
    chosen = jax.vmap(lambda subkey: jax.random.permutation(subkey, FBT)[:KC])(key_list)
    return chosen.reshape(N_TEAM, DB, KC).astype(jnp.int32)


def draw_col_owner(key, part):
    first_key, second_key = jax.random.split(jax.random.fold_in(key, 7))
    shuffle = jax.random.permutation(first_key, DB)
    busiest = jax.random.randint(second_key, (), 0, N_BLK)
    position = jnp.arange(DB, dtype=jnp.int32)
    others = (position - CAPC) % (N_BLK - 1)
    others = others + (others >= busiest).astype(jnp.int32)
    values = jnp.where(position < CAPC, busiest, others).astype(jnp.int32)
    return jnp.zeros((DB,), jnp.int32).at[shuffle].set(values)


def block_levels(stream_key, shape, cuts, smallest, top_value):
    factor_of, own = 1.0, jax.random.fold_in(stream_key, 6)
    for axis_at, parts in cuts:
        heights = jnp.exp(jax.random.uniform(jax.random.fold_in(own, axis_at), (parts,), jnp.float32, smallest / len(cuts), top_value / len(cuts)))
        factor_of = factor_of * jnp.repeat(heights, shape[axis_at] // parts).reshape([-1 if axis == axis_at else 1 for axis in range(len(shape))])
    return factor_of


def centred(rng, dims, spread, bound, shards=(), kind=jnp.bfloat16):
    loudness = block_levels(rng, dims, shards, -0.22, 0.18) if shards else 1.0
    array = jax.random.normal(rng, dims, jnp.float32) * spread * loudness
    return jnp.minimum(jnp.maximum(array, -bound), bound).astype(kind)


def setup_inputs(seed: int = 0) -> dict:
    seeds = jax.random.split(jax.random.key(seed), 5)
    hidden = centred(seeds[0], (TOKENS, FF), 1.0, 6.0, ((0, 8), (1, 4)))
    out_grad = centred(seeds[1], (TOKENS, D), (TOKENS ** -0.5), 0.1875, ((0, 8), (1, 4)))
    act_rows = draw_act_rows(jax.random.fold_in(seeds[4], 71), 0)
    col_owner = draw_col_owner(jax.random.fold_in(seeds[4], 71), 0)
    return {"hidden": hidden, "out_grad": out_grad, "act_rows": act_rows, "col_owner": col_owner}


epsilon = 1e-06

def owner_tables(col_owner):
    owners = jnp.arange(N_BLK, dtype=jnp.int32)
    onehot = (col_owner[:, None] == owners[None, :]).astype(jnp.int32)
    column_rank = lax.optimization_barrier(jnp.sum((jnp.cumsum(onehot, axis=0) - onehot) * onehot, axis=1))
    slot_ids = jnp.arange(CAPC, dtype=jnp.int32)
    matches = (col_owner[None, None, :] == owners[:, None, None]) & (column_rank[None, None, :] == slot_ids[None, :, None])
    owned_columns = lax.optimization_barrier(jnp.sum(matches.astype(jnp.int32) * jnp.arange(DB, dtype=jnp.int32)[None, None, :], axis=2))
    alive_mask = jnp.any(matches, axis=2)
    return (owned_columns, alive_mask)

def reference(hidden, out_grad, act_rows, col_owner):
    owned_columns, alive_mask = owner_tables(col_owner)
    team_width = FF // N_TEAM
    grad_blocks = out_grad.reshape(TOKENS, DB, BS)

    def one_owner(position):
        team_index = position // N_BLK
        owner_index = position % N_BLK
        team_hidden = lax.dynamic_slice_in_dim(hidden, (team_index * team_width).astype(jnp.int32), team_width, 1)
        team_hidden = team_hidden.reshape(TOKENS, FBT, BS)
        chosen = owned_columns[owner_index]
        living = alive_mask[owner_index]
        block_rows = act_rows[team_index][chosen]
        picked_hidden = jnp.take(team_hidden, block_rows.reshape(-1), axis=1).reshape(TOKENS, CAPC, KC, BS).astype(jnp.float32)
        picked_grad = jnp.take(grad_blocks, chosen, axis=1).astype(jnp.float32)
        blocks = jnp.einsum('ncki,ncj->ckij', picked_hidden, picked_grad)
        blocks = blocks * living.astype(jnp.float32)[:, None, None, None]
        return blocks.reshape(CAP, BS, BS)
    gradients = lax.map(one_owner, jnp.arange(N_TEAM * N_BLK, dtype=jnp.int32))
    gradients = gradients.reshape(N_TEAM, N_BLK, CAP, BS, BS)
    scores = jnp.sqrt(lax.optimization_barrier(jnp.mean(gradients * gradients, axis=(3, 4))) + epsilon)
    return (gradients, scores)
```

```python
import functools

import jax
import jax.numpy as jnp
from jax import lax
from jax.experimental import pallas as pl
from jax.experimental.pallas import tpu as pltpu
from jax.sharding import PartitionSpec as P

BS = 128
MESH = pl.DeviceIdType.MESH
CHUNKS = 4


epsilon = 1e-06


def owner_tables(col_owner, owners_count, capacity):
    column_blocks = col_owner.shape[0]
    owners = jnp.arange(owners_count, dtype=jnp.int32)
    onehot = (col_owner[:, None] == owners[None, :]).astype(jnp.int32)
    column_rank = jnp.sum((jnp.cumsum(onehot, axis=0) - onehot) * onehot, axis=1)
    slot_ids = jnp.arange(capacity, dtype=jnp.int32)
    matches = (col_owner[None, None, :] == owners[:, None, None]) & (
        column_rank[None, None, :] == slot_ids[None, :, None]
    )
    owned_all = jnp.sum(
        matches.astype(jnp.int32) * jnp.arange(column_blocks, dtype=jnp.int32)[None, None, :],
        axis=2,
    )
    return owned_all, jnp.any(matches, axis=2)


def gather_kernel(
    cols_ref, hid_ref, grad_ref, hfull, gfull, gz, gcol, snd, send_sem, recv_sem, local_sem
):
    teams = lax.axis_size("team")
    b, t, d = lax.axis_index("blk"), lax.axis_index("team"), lax.axis_index("dp")
    y, x = b // 2, b % 2
    panels, panel_rows, _ = hfull.shape
    part_rows = panel_rows // teams
    part_cols = grad_ref.shape[1]
    picks = cols_ref.shape[1]
    chunk = panel_rows // CHUNKS

    def plane(sy, sx, sd):
        oy = 1 - y if sy else y
        ox = 1 - x if sx else x
        return oy * 2 + ox, (1 - d if sd else d)

    def panel_of(sy, sx, sd):
        ob, od = plane(sy, sx, sd)
        return ob * 2 + od

    def device(sy, sx, sd):
        ob, od = plane(sy, sx, sd)
        return (ob, t, od)

    mine = panel_of(0, 0, 0)
    flips = [(sy, sx, sd) for sy in (0, 1) for sx in (0, 1) for sd in (0, 1)][1:]

    barrier = pltpu.get_barrier_semaphore()
    for flip in flips:
        pl.semaphore_signal(barrier, inc=1, device_id=device(*flip), device_id_type=MESH)
    for s in range(1, teams):
        pl.semaphore_signal(
            barrier, inc=1, device_id=(b, (t + s) % teams, d), device_id_type=MESH
        )
    pl.semaphore_wait(barrier, len(flips) + teams - 1)

    counter = [0]

    def remote(src, dst, target, slot=None):
        if slot is None:
            slot = counter[0]
            counter[0] += 1
        return pltpu.make_async_remote_copy(
            src_ref=src,
            dst_ref=dst,
            send_sem=send_sem.at[slot],
            recv_sem=recv_sem.at[slot],
            device_id=target,
            device_id_type=MESH,
        )

    sent = []

    def rows_of(c):
        return pl.ds(c * chunk, chunk)

    def send_own(flip, c):
        copy = remote(hid_ref.at[rows_of(c)], hfull.at[mine, rows_of(c)], device(*flip))
        copy.start()
        sent.append(copy)
        return copy

    def forward(panel, flip, c):
        piece = hfull.at[panel, rows_of(c)]
        copy = remote(piece, piece, device(*flip))
        copy.start()
        sent.append(copy)
        return copy

    def part(k):
        return pl.ds(k * part_rows, part_rows)

    def quarter(k):
        return pl.ds(k * part_cols, part_cols)

    own_grad = pltpu.make_async_copy(
        grad_ref.at[part(t)], gz.at[:, quarter(t)], local_sem.at[0]
    )
    stage1 = []
    for s in range(1, teams):
        target = (t + s) % teams
        copy = remote(grad_ref.at[part(target)], gz.at[:, quarter(t)], (b, target, d))
        copy.start()
        stage1.append(copy)
        sent.append(copy)
    own_grad.start()

    order_x = list(range(CHUNKS))
    order_y = order_x[CHUNKS // 2 :] + order_x[: CHUNKS // 2]
    X, Y, SIB = (0, 1, 0), (1, 0, 0), (0, 0, 1)
    from_x, from_y, from_sib = {}, {}, []
    from_x[order_x[0]] = send_own(X, order_x[0])
    from_y[order_y[0]] = send_own(Y, order_y[0])
    own_hidden = pltpu.make_async_copy(hid_ref, hfull.at[mine], local_sem.at[1])
    own_hidden.start()

    own_grad.wait()
    for copy in stage1:
        copy.wait_recv()

    for c in range(gcol.shape[0]):
        gcol[c] = gz[:, c * BS : (c + 1) * BS]

    def pick(p, carry):
        for j in range(picks):
            snd[p, :, j * BS : (j + 1) * BS] = gcol[cols_ref[p, j]]
        return carry

    lax.fori_loop(0, panels, pick, 0)
    stage2 = []
    for flip in flips:
        copy = remote(snd.at[panel_of(*flip)], gfull.at[mine, part(t)], device(*flip))
        copy.start()
        stage2.append(copy)
        sent.append(copy)
    own_pick = pltpu.make_async_copy(snd.at[mine], gfull.at[mine, part(t)], local_sem.at[2])
    own_pick.start()

    for i in range(1, CHUNKS):
        from_x[order_x[i]] = send_own(X, order_x[i])
        from_y[order_y[i]] = send_own(Y, order_y[i])
    for c in range(CHUNKS):
        from_sib.append(send_own(SIB, c))

    own_pick.wait()
    for copy in stage2:
        copy.wait_recv()

    chain_base = counter[0]
    counter[0] += 2 * (teams - 1)

    def chain(up, k, shard, target):
        piece = gfull.at[:, part(shard)]
        slot = chain_base + (k if up else teams - 1 + k)
        return remote(piece, piece, (b, target, d), slot)

    def chain_send(k, wait):
        @pl.when((t < teams - 1) & (t - k >= 0))
        def _():
            copy = chain(True, k, t - k, t + 1)
            copy.wait_send() if wait else copy.start()

        @pl.when((t > 0) & (t + k < teams))
        def _():
            copy = chain(False, k, t + k, t - 1)
            copy.wait_send() if wait else copy.start()

    def chain_recv(k):
        @pl.when(t - 1 - k >= 0)
        def _():
            chain(True, k, t - 1 - k, t - 1).wait_recv()

        @pl.when(t + 1 + k < teams)
        def _():
            chain(False, k, t + 1 + k, t + 1).wait_recv()

    chain_send(0, False)

    panel_x, panel_y, panel_xy = panel_of(*X), panel_of(*Y), panel_of(1, 1, 0)
    from_xy = {}
    steps = 0
    for i in range(CHUNKS):
        cx, cy = order_x[i], order_y[i]
        from_x[cx].wait_recv()
        if i < CHUNKS // 2:
            from_xy[cx] = forward(panel_x, Y, cx)
        from_sib.append(forward(panel_x, SIB, cx))
        from_y[cy].wait_recv()
        if i < CHUNKS // 2:
            from_xy[cy] = forward(panel_y, X, cy)
        from_sib.append(forward(panel_y, SIB, cy))
        if i % 2 == 1 and steps < teams - 1:
            chain_recv(steps)
            steps += 1
            if steps < teams - 1:
                chain_send(steps, False)
    for c in order_x:
        c = order_x[c // 2] if c % 2 == 0 else order_y[c // 2]
        from_xy[c].wait_recv()
        from_sib.append(forward(panel_xy, SIB, c))
    while steps < teams - 1:
        chain_recv(steps)
        steps += 1
        if steps < teams - 1:
            chain_send(steps, False)
    for copy in from_sib:
        copy.wait_recv()
    for copy in sent:
        copy.wait_send()
    for k in range(teams - 1):
        chain_send(k, True)
    own_hidden.wait()


def gather(columns, hidden, out_grad, panels):
    teams = lax.axis_size("team")
    panel_rows, units = hidden.shape
    picks = columns.shape[1]
    copies = (teams - 1) + 7 + 3 * CHUNKS + 4 * CHUNKS + 2 * (teams - 1)
    hbm = pl.BlockSpec(memory_space=pl.ANY)
    return pl.pallas_call(
        gather_kernel,
        out_shape=(
            jax.ShapeDtypeStruct((panels, panel_rows, units), hidden.dtype),
            jax.ShapeDtypeStruct((panels, panel_rows, picks * BS), out_grad.dtype),
        ),
        in_specs=[pl.BlockSpec(memory_space=pltpu.SMEM), hbm, hbm],
        out_specs=(hbm, hbm),
        scratch_shapes=[
            pltpu.VMEM((panel_rows // teams, teams * out_grad.shape[1]), out_grad.dtype),
            pltpu.VMEM(
                (teams * out_grad.shape[1] // BS, panel_rows // teams, BS), out_grad.dtype
            ),
            pltpu.VMEM((panels, panel_rows // teams, picks * BS), out_grad.dtype),
            pltpu.SemaphoreType.DMA((copies,)),
            pltpu.SemaphoreType.DMA((copies,)),
            pltpu.SemaphoreType.DMA((3,)),
        ],
        compiler_params=pltpu.CompilerParams(collective_id=0, has_side_effects=True),
    )(columns, hidden, out_grad)


def block_kernel(rows_ref, alive_ref, h_ref, g_ref, out_ref, ssq_ref):
    j = pl.program_id(0)
    per_column = out_ref.shape[0]
    scale = alive_ref[j].astype(jnp.float32)
    g_t = g_ref[...].T
    for k in range(0, per_column, 2):
        pair = []
        for i in (k, k + 1):
            r = rows_ref[j * per_column + i]
            pair.append(h_ref[:, pl.ds(pl.multiple_of(r * BS, BS), BS)])
        both = jnp.dot(
            g_t, jnp.concatenate(pair, axis=1), preferred_element_type=jnp.float32
        )
        for i in range(2):
            block = both[:, i * BS : (i + 1) * BS].T * scale
            out_ref[k + i] = block
            ssq_ref[0, k + i, :] = jnp.sum(block * block, axis=0)


def blocks(rows, alive, hidden, grad):
    picks = alive.shape[0]
    per_column = rows.shape[0] // picks
    tokens, units = hidden.shape
    return pl.pallas_call(
        block_kernel,
        out_shape=(
            jax.ShapeDtypeStruct((picks * per_column, BS, BS), jnp.float32),
            jax.ShapeDtypeStruct((picks, per_column, BS), jnp.float32),
        ),
        grid_spec=pltpu.PrefetchScalarGridSpec(
            num_scalar_prefetch=2,
            grid=(picks,),
            in_specs=[
                pl.BlockSpec(
                    (tokens, units), lambda j, *_: (0, 0), pipeline_mode=pl.Buffered(1)
                ),
                pl.BlockSpec((tokens, BS), lambda j, *_: (0, j)),
            ],
            out_specs=(
                pl.BlockSpec((per_column, BS, BS), lambda j, *_: (j, 0, 0)),
                pl.BlockSpec((1, per_column, BS), lambda j, *_: (j, 0, 0)),
            ),
        ),
        compiler_params=pltpu.CompilerParams(dimension_semantics=("arbitrary",)),
    )(rows, alive, hidden, grad)


def in_plane(hidden, out_grad, act_rows, col_owner):
    owners_count, cores = lax.axis_size("blk"), lax.axis_size("dp")
    column_blocks = col_owner.shape[0]
    capacity = min(3 * column_blocks // (2 * owners_count), 3 * column_blocks // 4)
    owned_all, alive_all = owner_tables(col_owner, owners_count, capacity)
    panels = owners_count * cores
    picks = capacity // cores
    columns = owned_all.reshape(panels, picks)
    mine = lax.axis_index("blk") * cores + lax.axis_index("dp")
    columns_mine = lax.dynamic_index_in_dim(columns, mine, 0, keepdims=False)
    alive_mine = lax.dynamic_index_in_dim(
        alive_all.reshape(panels, picks), mine, 0, keepdims=False
    ).astype(jnp.int32)
    rows = jnp.take(act_rows[0], columns_mine, axis=0).reshape(-1)
    hidden_all, grad_mine = gather(columns, hidden, out_grad, panels)
    tokens = panels * hidden.shape[0]
    gradients, ssq = blocks(
        rows,
        alive_mine,
        hidden_all.reshape(tokens, hidden.shape[1]),
        grad_mine.reshape(tokens, picks * BS),
    )
    mean = jnp.sum(ssq, axis=2).reshape(-1) * (1.0 / (BS * BS))
    scores = jnp.sqrt(mean + epsilon)
    return (gradients[None, None], scores[None, None])


def on_device(hidden, out_grad, act_rows, col_owner):
    owners_count = lax.axis_size("blk")
    owner_index = lax.axis_index("blk")
    column_blocks = col_owner.shape[0]
    capacity = min(3 * column_blocks // (2 * owners_count), 3 * column_blocks // 4)
    per_column = act_rows.shape[2]
    owned_all, alive_all = owner_tables(col_owner, owners_count, capacity)
    owned_mine = lax.dynamic_index_in_dim(owned_all, owner_index, 0, keepdims=False)
    alive_mine = lax.dynamic_index_in_dim(alive_all, owner_index, 0, keepdims=False)
    block_rows = jnp.take(act_rows[0], owned_mine, axis=0).reshape(-1)
    grad_full = lax.all_gather(out_grad, "team", axis=1, tiled=True)
    grad_mask = alive_mine.astype(jnp.bfloat16)[None, :, None]
    hidden_piece = lax.all_gather(hidden, "blk", axis=0, tiled=True)
    grad_piece = lax.all_gather(grad_full, "blk", axis=0, tiled=True)
    count_rows = grad_piece.shape[0]
    picked_grad = (
        jnp.take(grad_piece.reshape(count_rows, column_blocks, BS), owned_mine, axis=1) * grad_mask
    )
    hidden_blocks = hidden_piece.reshape(count_rows, -1, BS)
    picked_hidden = jnp.take(hidden_blocks, block_rows, axis=1).reshape(
        count_rows, capacity, per_column, BS
    )
    partial_value = jnp.einsum(
        "ncki,ncj->ckij", picked_hidden, picked_grad, preferred_element_type=jnp.float32
    )
    partial_value = partial_value.reshape(capacity * per_column, BS, BS)
    gradients = lax.psum_scatter(partial_value, "dp", scatter_dimension=0, tiled=True)
    scores = jnp.sqrt(jnp.mean(gradients * gradients, axis=(1, 2)) + epsilon)
    return (gradients[None, None], scores[None, None])


def solution(mesh):
    in_specs = (P(("blk", "dp"), "team"), P(("blk", "dp"), "team"), P("team", None, None), P())
    out_specs = (P("team", "blk", "dp", None, None), P("team", "blk", "dp"))
    square = mesh.shape["blk"] == 4 and mesh.shape["dp"] == 2
    return jax.shard_map(
        in_plane if square else on_device,
        mesh=mesh,
        in_specs=in_specs,
        out_specs=out_specs,
        check_vma=False,
    )
```

```python
import functools

import jax
import jax.numpy as jnp
from jax import lax
from jax.experimental import pallas as pl
from jax.experimental.pallas import tpu as pltpu
from jax.sharding import PartitionSpec as P

BS = 128
MESH = pl.DeviceIdType.MESH
CHUNKS = 4


epsilon = 1e-06


def owner_tables(col_owner, owners_count, capacity):
    column_blocks = col_owner.shape[0]
    owners = jnp.arange(owners_count, dtype=jnp.int32)
    onehot = (col_owner[:, None] == owners[None, :]).astype(jnp.int32)
    column_rank = jnp.sum((jnp.cumsum(onehot, axis=0) - onehot) * onehot, axis=1)
    slot_ids = jnp.arange(capacity, dtype=jnp.int32)
    matches = (col_owner[None, None, :] == owners[:, None, None]) & (
        column_rank[None, None, :] == slot_ids[None, :, None]
    )
    owned_all = jnp.sum(
        matches.astype(jnp.int32) * jnp.arange(column_blocks, dtype=jnp.int32)[None, None, :],
        axis=2,
    )
    return owned_all, jnp.any(matches, axis=2)


def gather_kernel(
    cols_ref,
    rows_ref,
    hid_ref,
    grad_ref,
    sums_ref,
    far_ref,
    far_grad,
    near,
    sums,
    gfull,
    gz,
    gcol,
    snd,
    send_sem,
    recv_sem,
    local_sem,
    block_sem,
    sums_sem,
):
    teams = lax.axis_size("team")
    b, t, d = lax.axis_index("blk"), lax.axis_index("team"), lax.axis_index("dp")
    y, x = b // 2, b % 2
    panels, panel_rows, _ = gfull.shape
    units = near.shape[0]
    near_panels = near.shape[1] // panel_rows
    part_rows = panel_rows // teams
    part_cols = grad_ref.shape[1]
    picks = cols_ref.shape[1]
    chunk = units // CHUNKS

    def plane(sy, sx, sd):
        oy = 1 - y if sy else y
        ox = 1 - x if sx else x
        return oy * 2 + ox, (1 - d if sd else d)

    def panel_of(sy, sx, sd):
        ob, od = plane(sy, sx, sd)
        return ob * 2 + od

    def device(sy, sx, sd):
        ob, od = plane(sy, sx, sd)
        return (ob, t, od)

    def slot_of(flip):
        return (flip[0] * 2 + flip[1]) * 2 + flip[2]

    mine = panel_of(0, 0, 0)
    flips = [(sy, sx, sd) for sy in (0, 1) for sx in (0, 1) for sd in (0, 1)][1:]

    own_blocks = [
        pltpu.make_async_copy(
            hid_ref.at[:, pl.ds(r * BS, BS)],
            near.at[r, pl.ds(0, panel_rows)],
            block_sem.at[r],
        )
        for r in range(units)
    ]
    own_ready = set()

    barrier = pltpu.get_barrier_semaphore()
    for flip in flips:
        pl.semaphore_signal(barrier, inc=1, device_id=device(*flip), device_id_type=MESH)
    for s in range(1, teams):
        pl.semaphore_signal(
            barrier, inc=1, device_id=(b, (t + s) % teams, d), device_id_type=MESH
        )
    pl.semaphore_wait(barrier, len(flips) + teams - 1)

    counter = [0]

    def remote(src, dst, target, slot=None):
        if slot is None:
            slot = counter[0]
            counter[0] += 1
        return pltpu.make_async_remote_copy(
            src_ref=src,
            dst_ref=dst,
            send_sem=send_sem.at[slot],
            recv_sem=recv_sem.at[slot],
            device_id=target,
            device_id_type=MESH,
        )

    sent = []

    def piece(slot, c):
        held = pl.ds(c * chunk, chunk)
        if slot < near_panels:
            return near.at[held, pl.ds(slot * panel_rows, panel_rows)]
        return far_ref.at[held, pl.ds((slot - near_panels) * panel_rows, panel_rows)]

    def forward(source, flip, c):
        there = tuple(one ^ two for one, two in zip(source, flip))
        copy = remote(piece(slot_of(source), c), piece(slot_of(there), c), device(*flip))
        copy.start()
        sent.append(copy)
        return copy

    def send_own(flip, c):
        if c not in own_ready:
            own_ready.add(c)
            for r in range(c * chunk, (c + 1) * chunk):
                own_blocks[r].wait()
        return forward((0, 0, 0), flip, c)

    def part(k):
        return pl.ds(k * part_rows, part_rows)

    def quarter(k):
        return pl.ds(k * part_cols, part_cols)

    own_grad = pltpu.make_async_copy(
        grad_ref.at[part(t)], gz.at[:, quarter(t)], local_sem.at[0]
    )
    stage1 = []
    for s in range(1, teams):
        target = (t + s) % teams
        copy = remote(grad_ref.at[part(target)], gz.at[:, quarter(t)], (b, target, d))
        copy.start()
        stage1.append(copy)
        sent.append(copy)
    own_grad.start()

    X, Y, XY, SIB = (0, 1, 0), (1, 0, 0), (1, 1, 0), (0, 0, 1)
    order_x = list(range(CHUNKS))
    order_y = order_x[CHUNKS // 2 :] + order_x[: CHUNKS // 2]
    for pair in zip(order_x[: CHUNKS // 2], order_y[: CHUNKS // 2]):
        for c in pair:
            for r in range(c * chunk, (c + 1) * chunk):
                own_blocks[r].start()
    from_x, from_y, from_sib = {}, {}, []
    from_x[order_x[0]] = send_own(X, order_x[0])
    from_y[order_y[0]] = send_own(Y, order_y[0])

    own_grad.wait()
    for copy in stage1:
        copy.wait_recv()

    for c in range(gcol.shape[0]):
        gcol[c] = gz[:, c * BS : (c + 1) * BS]

    def pick(p, carry):
        for j in range(picks):
            snd[p, :, j * BS : (j + 1) * BS] = gcol[cols_ref[p, j]]
        return carry

    lax.fori_loop(0, panels, pick, 0)
    stage2 = []
    for flip in flips:
        copy = remote(snd.at[panel_of(*flip)], gfull.at[slot_of(flip), part(t)], device(*flip))
        copy.start()
        stage2.append(copy)
        sent.append(copy)
    own_pick = pltpu.make_async_copy(snd.at[mine], gfull.at[0, part(t)], local_sem.at[2])
    own_pick.start()

    for i in range(1, CHUNKS):
        from_x[order_x[i]] = send_own(X, order_x[i])
        from_y[order_y[i]] = send_own(Y, order_y[i])
    for c in range(CHUNKS):
        from_sib.append(send_own(SIB, c))

    own_pick.wait()
    for copy in stage2:
        copy.wait_recv()

    chain_base = counter[0]
    counter[0] += 2 * (teams - 1)

    def chain(up, k, shard, target):
        subset = gfull.at[:, part(shard)]
        slot = chain_base + (k if up else teams - 1 + k)
        return remote(subset, subset, (b, target, d), slot)

    def chain_send(k, wait):
        @pl.when((t < teams - 1) & (t - k >= 0))
        def _():
            copy = chain(True, k, t - k, t + 1)
            copy.wait_send() if wait else copy.start()

        @pl.when((t > 0) & (t + k < teams))
        def _():
            copy = chain(False, k, t + k, t - 1)
            copy.wait_send() if wait else copy.start()

    def chain_recv(k):
        @pl.when(t - 1 - k >= 0)
        def _():
            chain(True, k, t - 1 - k, t - 1).wait_recv()

        @pl.when(t + 1 + k < teams)
        def _():
            chain(False, k, t + 1 + k, t + 1).wait_recv()

    chain_send(0, False)

    from_xy = {}
    steps = 0
    for i in range(CHUNKS):
        cx, cy = order_x[i], order_y[i]
        from_x[cx].wait_recv()
        if i < CHUNKS // 2:
            from_xy[cx] = forward(X, Y, cx)
        from_sib.append(forward(X, SIB, cx))
        from_y[cy].wait_recv()
        if i < CHUNKS // 2:
            from_xy[cy] = forward(Y, X, cy)
        from_sib.append(forward(Y, SIB, cy))
        if i % 2 == 1 and steps < teams - 1:
            chain_recv(steps)
            steps += 1
            if steps < teams - 1:
                chain_send(steps, False)
    arrivals = [c for pair in zip(order_x[: CHUNKS // 2], order_y[: CHUNKS // 2]) for c in pair]

    def pass_on(c):
        from_xy[c].wait_recv()
        from_far.append(forward(XY, SIB, c))

    from_far = []
    for c in arrivals[: CHUNKS // 2]:
        pass_on(c)
    while steps < teams - 1:
        chain_recv(steps)
        steps += 1
        if steps < teams - 1:
            chain_send(steps, False)
    give_grad = pltpu.make_async_copy(
        gfull.at[pl.ds(near_panels, panels - near_panels)], far_grad, local_sem.at[1]
    )
    give_grad.start()
    for copy in from_sib:
        copy.wait_recv()

    pairs = sums.shape[1]

    def give_sums(j):
        return pltpu.make_async_copy(sums.at[j], sums_ref.at[j], sums_sem.at[j])

    def column(j, carry):
        lanes = pl.ds(pl.multiple_of(j * BS, BS), BS)
        g_t = gfull[:near_panels, :, lanes].reshape(near_panels * panel_rows, BS).T
        for k in range(pairs):
            s = (j * pairs + k) * 2
            both = jnp.concatenate([near[rows_ref[s]], near[rows_ref[s + 1]]], axis=1)
            sums[j, k] = jnp.dot(g_t, both, preferred_element_type=jnp.float32)
        give_sums(j).start()
        return carry

    lax.fori_loop(0, picks, column, 0)
    for c in arrivals[CHUNKS // 2 :]:
        pass_on(c)
    for copy in from_far:
        copy.wait_recv()
    for copy in sent:
        copy.wait_send()
    for k in range(teams - 1):
        chain_send(k, True)
    give_grad.wait()
    for j in range(picks):
        give_sums(j).wait()


def gather(columns, rows, hidden, out_grad, panels):
    teams = lax.axis_size("team")
    panel_rows, units = hidden.shape
    picks = columns.shape[1]
    pairs = rows.shape[0] // picks // 2
    near, far = panels - 2, 2
    copies = (teams - 1) + 7 + 3 * CHUNKS + 4 * CHUNKS + 2 * (teams - 1)
    hbm = pl.BlockSpec(memory_space=pl.ANY)
    smem = pl.BlockSpec(memory_space=pltpu.SMEM)
    return pl.pallas_call(
        gather_kernel,
        out_shape=(
            jax.ShapeDtypeStruct((picks, pairs, BS, 2 * BS), jnp.float32),
            jax.ShapeDtypeStruct((units // BS, far * panel_rows, BS), hidden.dtype),
            jax.ShapeDtypeStruct((far, panel_rows, picks * BS), out_grad.dtype),
        ),
        in_specs=[smem, smem, hbm, hbm],
        out_specs=(hbm, hbm, hbm),
        scratch_shapes=[
            pltpu.VMEM((units // BS, near * panel_rows, BS), hidden.dtype),
            pltpu.VMEM((picks, pairs, BS, 2 * BS), jnp.float32),
            pltpu.VMEM((panels, panel_rows, picks * BS), out_grad.dtype),
            pltpu.VMEM((panel_rows // teams, teams * out_grad.shape[1]), out_grad.dtype),
            pltpu.VMEM(
                (teams * out_grad.shape[1] // BS, panel_rows // teams, BS), out_grad.dtype
            ),
            pltpu.VMEM((panels, panel_rows // teams, picks * BS), out_grad.dtype),
            pltpu.SemaphoreType.DMA((copies,)),
            pltpu.SemaphoreType.DMA((copies,)),
            pltpu.SemaphoreType.DMA((3,)),
            pltpu.SemaphoreType.DMA((units // BS,)),
            pltpu.SemaphoreType.DMA((picks,)),
        ],
        compiler_params=pltpu.CompilerParams(collective_id=0, has_side_effects=True),
    )(columns, rows, hidden, out_grad)


def block_kernel(rows_ref, alive_ref, sums_ref, h_ref, g_ref, out_ref, ssq_ref):
    j = pl.program_id(0)
    per_column = out_ref.shape[0]
    scale = alive_ref[j].astype(jnp.float32)
    g_t = g_ref[...].T
    for k in range(0, per_column, 2):
        s = j * per_column + k
        pair = jnp.concatenate([h_ref[rows_ref[s]], h_ref[rows_ref[s + 1]]], axis=1)
        both = sums_ref[0, k // 2] + jnp.dot(g_t, pair, preferred_element_type=jnp.float32)
        for i in range(2):
            block = both[:, i * BS : (i + 1) * BS].T * scale
            out_ref[k + i] = block
            ssq_ref[0, k + i, :] = jnp.sum(block * block, axis=0)


def blocks(rows, alive, sums, hidden, grad):
    picks, pairs = sums.shape[:2]
    per_column = pairs * 2
    tokens = grad.shape[0]
    return pl.pallas_call(
        block_kernel,
        out_shape=(
            jax.ShapeDtypeStruct((picks * per_column, BS, BS), jnp.float32),
            jax.ShapeDtypeStruct((picks, per_column, BS), jnp.float32),
        ),
        grid_spec=pltpu.PrefetchScalarGridSpec(
            num_scalar_prefetch=2,
            grid=(picks,),
            in_specs=[
                pl.BlockSpec((1, pairs, BS, 2 * BS), lambda j, *_: (j, 0, 0, 0)),
                pl.BlockSpec(
                    hidden.shape, lambda j, *_: (0, 0, 0), pipeline_mode=pl.Buffered(1)
                ),
                pl.BlockSpec((tokens, BS), lambda j, *_: (0, j)),
            ],
            out_specs=(
                pl.BlockSpec((per_column, BS, BS), lambda j, *_: (j, 0, 0)),
                pl.BlockSpec((1, per_column, BS), lambda j, *_: (j, 0, 0)),
            ),
        ),
        compiler_params=pltpu.CompilerParams(dimension_semantics=("arbitrary",)),
    )(rows, alive, sums, hidden, grad)


def in_plane(hidden, out_grad, act_rows, col_owner):
    owners_count, cores = lax.axis_size("blk"), lax.axis_size("dp")
    column_blocks = col_owner.shape[0]
    capacity = min(3 * column_blocks // (2 * owners_count), 3 * column_blocks // 4)
    owned_all, alive_all = owner_tables(col_owner, owners_count, capacity)
    panels = owners_count * cores
    picks = capacity // cores
    columns = owned_all.reshape(panels, picks)
    mine = lax.axis_index("blk") * cores + lax.axis_index("dp")
    columns_mine = lax.dynamic_index_in_dim(columns, mine, 0, keepdims=False)
    alive_mine = lax.dynamic_index_in_dim(
        alive_all.reshape(panels, picks), mine, 0, keepdims=False
    ).astype(jnp.int32)
    rows = jnp.take(act_rows[0], columns_mine, axis=0).reshape(-1)
    sums, far_hidden, far_grad = gather(columns, rows, hidden, out_grad, panels)
    gradients, ssq = blocks(
        rows, alive_mine, sums, far_hidden, far_grad.reshape(-1, picks * BS)
    )
    mean = jnp.sum(ssq, axis=2).reshape(-1) * (1.0 / (BS * BS))
    scores = jnp.sqrt(mean + epsilon)
    return (gradients[None, None], scores[None, None])


def on_device(hidden, out_grad, act_rows, col_owner):
    owners_count = lax.axis_size("blk")
    owner_index = lax.axis_index("blk")
    column_blocks = col_owner.shape[0]
    capacity = min(3 * column_blocks // (2 * owners_count), 3 * column_blocks // 4)
    per_column = act_rows.shape[2]
    owned_all, alive_all = owner_tables(col_owner, owners_count, capacity)
    owned_mine = lax.dynamic_index_in_dim(owned_all, owner_index, 0, keepdims=False)
    alive_mine = lax.dynamic_index_in_dim(alive_all, owner_index, 0, keepdims=False)
    block_rows = jnp.take(act_rows[0], owned_mine, axis=0).reshape(-1)
    grad_full = lax.all_gather(out_grad, "team", axis=1, tiled=True)
    grad_mask = alive_mine.astype(jnp.bfloat16)[None, :, None]
    hidden_piece = lax.all_gather(hidden, "blk", axis=0, tiled=True)
    grad_piece = lax.all_gather(grad_full, "blk", axis=0, tiled=True)
    count_rows = grad_piece.shape[0]
    picked_grad = (
        jnp.take(grad_piece.reshape(count_rows, column_blocks, BS), owned_mine, axis=1) * grad_mask
    )
    hidden_blocks = hidden_piece.reshape(count_rows, -1, BS)
    picked_hidden = jnp.take(hidden_blocks, block_rows, axis=1).reshape(
        count_rows, capacity, per_column, BS
    )
    partial_value = jnp.einsum(
        "ncki,ncj->ckij", picked_hidden, picked_grad, preferred_element_type=jnp.float32
    )
    partial_value = partial_value.reshape(capacity * per_column, BS, BS)
    gradients = lax.psum_scatter(partial_value, "dp", scatter_dimension=0, tiled=True)
    scores = jnp.sqrt(jnp.mean(gradients * gradients, axis=(1, 2)) + epsilon)
    return (gradients[None, None], scores[None, None])


def solution(mesh):
    in_specs = (P(("blk", "dp"), "team"), P(("blk", "dp"), "team"), P("team", None, None), P())
    out_specs = (P("team", "blk", "dp", None, None), P("team", "blk", "dp"))
    square = mesh.shape["blk"] == 4 and mesh.shape["dp"] == 2
    return jax.shard_map(
        in_plane if square else on_device,
        mesh=mesh,
        in_specs=in_specs,
        out_specs=out_specs,
        check_vma=False,
    )
```

```python
import functools

import jax
import jax.numpy as jnp
from jax import lax
from jax.experimental import pallas as pl
from jax.experimental.pallas import tpu as pltpu
from jax.sharding import PartitionSpec as P

BS = 128
MESH = pl.DeviceIdType.MESH
CHUNKS = 4
HALVES = 2


epsilon = 1e-06


def owner_tables(col_owner, owners_count, capacity):
    column_blocks = col_owner.shape[0]
    owners = jnp.arange(owners_count, dtype=jnp.int32)
    onehot = (col_owner[:, None] == owners[None, :]).astype(jnp.int32)
    column_rank = jnp.sum((jnp.cumsum(onehot, axis=0) - onehot) * onehot, axis=1)
    slot_ids = jnp.arange(capacity, dtype=jnp.int32)
    matches = (col_owner[None, None, :] == owners[:, None, None]) & (
        column_rank[None, None, :] == slot_ids[None, :, None]
    )
    owned_all = jnp.sum(
        matches.astype(jnp.int32) * jnp.arange(column_blocks, dtype=jnp.int32)[None, None, :],
        axis=2,
    )
    return owned_all, jnp.any(matches, axis=2)


def gather_kernel(
    cols_ref, hid_ref, grad_ref, hfull, gfull, gz, gcol, snd, send_sem, recv_sem, local_sem
):
    teams = lax.axis_size("team")
    b, t, d = lax.axis_index("blk"), lax.axis_index("team"), lax.axis_index("dp")
    y, x = b // 2, b % 2
    panels, panel_rows, _ = hfull.shape
    part_rows = panel_rows // teams
    part_cols = grad_ref.shape[1]
    picks = cols_ref.shape[1]
    chunk = panel_rows // CHUNKS

    def plane(sy, sx, sd):
        oy = 1 - y if sy else y
        ox = 1 - x if sx else x
        return oy * 2 + ox, (1 - d if sd else d)

    def panel_of(sy, sx, sd):
        ob, od = plane(sy, sx, sd)
        return ob * 2 + od

    def device(sy, sx, sd):
        ob, od = plane(sy, sx, sd)
        return (ob, t, od)

    mine = panel_of(0, 0, 0)
    flips = [(sy, sx, sd) for sy in (0, 1) for sx in (0, 1) for sd in (0, 1)][1:]

    barrier = pltpu.get_barrier_semaphore()
    for flip in flips:
        pl.semaphore_signal(barrier, inc=1, device_id=device(*flip), device_id_type=MESH)
    for s in range(1, teams):
        pl.semaphore_signal(
            barrier, inc=1, device_id=(b, (t + s) % teams, d), device_id_type=MESH
        )
    pl.semaphore_wait(barrier, len(flips) + teams - 1)

    counter = [0]

    def remote(src, dst, target, slot=None):
        if slot is None:
            slot = counter[0]
            counter[0] += 1
        return pltpu.make_async_remote_copy(
            src_ref=src,
            dst_ref=dst,
            send_sem=send_sem.at[slot],
            recv_sem=recv_sem.at[slot],
            device_id=target,
            device_id_type=MESH,
        )

    sent = []

    def rows_of(c):
        return pl.ds(c * chunk, chunk)

    def send_own(flip, c):
        copy = remote(hid_ref.at[rows_of(c)], hfull.at[mine, rows_of(c)], device(*flip))
        copy.start()
        sent.append(copy)
        return copy

    def forward(panel, flip, c):
        piece = hfull.at[panel, rows_of(c)]
        copy = remote(piece, piece, device(*flip))
        copy.start()
        sent.append(copy)
        return copy

    half_rows = part_rows // HALVES

    def part(k, half):
        return pl.ds(k * part_rows + half * half_rows, half_rows)

    def held(half):
        return pl.ds(half * half_rows, half_rows)

    def quarter(k):
        return pl.ds(k * part_cols, part_cols)

    own_grad, stage1 = [], []
    for half in range(HALVES):
        for s in range(1, teams):
            target = (t + s) % teams
            copy = remote(
                grad_ref.at[part(target, half)],
                gz.at[held(half), quarter(t)],
                (b, target, d),
            )
            copy.start()
            stage1.append(copy)
            sent.append(copy)
        own_grad.append(
            pltpu.make_async_copy(
                grad_ref.at[part(t, half)],
                gz.at[held(half), quarter(t)],
                local_sem.at[1 + half],
            )
        )
        own_grad[half].start()

    order_x = list(range(CHUNKS))
    order_y = order_x[CHUNKS // 2 :] + order_x[: CHUNKS // 2]
    X, Y, SIB = (0, 1, 0), (1, 0, 0), (0, 0, 1)
    from_x, from_y, from_sib = {}, {}, []
    from_x[order_x[0]] = send_own(X, order_x[0])
    from_y[order_y[0]] = send_own(Y, order_y[0])
    own_hidden = pltpu.make_async_copy(hid_ref, hfull.at[mine], local_sem.at[0])
    own_hidden.start()

    own_pick, stage2 = [], []
    for half in range(HALVES):
        own_grad[half].wait()
        for copy in stage1[half * (teams - 1) : (half + 1) * (teams - 1)]:
            copy.wait_recv()
        rows = slice(half * half_rows, (half + 1) * half_rows)
        for c in range(gcol.shape[1]):
            gcol[half, c] = gz[rows, c * BS : (c + 1) * BS]

        def pick(p, carry):
            for j in range(picks):
                snd[half, p, :, j * BS : (j + 1) * BS] = gcol[half, cols_ref[p, j]]
            return carry

        lax.fori_loop(0, panels, pick, 0)
        landing = gfull.at[mine, part(t, half)]
        for flip in flips:
            copy = remote(snd.at[half, panel_of(*flip)], landing, device(*flip))
            copy.start()
            stage2.append(copy)
            sent.append(copy)
        own_pick.append(
            pltpu.make_async_copy(
                snd.at[half, mine], landing, local_sem.at[1 + HALVES + half]
            )
        )
        own_pick[half].start()

    for i in range(1, CHUNKS):
        from_x[order_x[i]] = send_own(X, order_x[i])
        from_y[order_y[i]] = send_own(Y, order_y[i])
    for c in range(CHUNKS):
        from_sib.append(send_own(SIB, c))

    chain_base = counter[0]
    counter[0] += 2 * (teams - 1) * HALVES

    def chain(up, k, shard, target, half):
        piece = gfull.at[:, part(shard, half)]
        step = k if up else teams - 1 + k
        return remote(piece, piece, (b, target, d), chain_base + step * HALVES + half)

    def chain_send(k, half, wait):
        @pl.when((t < teams - 1) & (t - k >= 0))
        def _():
            copy = chain(True, k, t - k, t + 1, half)
            copy.wait_send() if wait else copy.start()

        @pl.when((t > 0) & (t + k < teams))
        def _():
            copy = chain(False, k, t + k, t - 1, half)
            copy.wait_send() if wait else copy.start()

    def chain_recv(k, half):
        @pl.when(t - 1 - k >= 0)
        def _():
            chain(True, k, t - 1 - k, t - 1, half).wait_recv()

        @pl.when(t + 1 + k < teams)
        def _():
            chain(False, k, t + 1 + k, t + 1, half).wait_recv()

    def chain_step(k):
        for half in range(HALVES):
            chain_recv(k, half)
            if k < teams - 2:
                chain_send(k + 1, half, False)

    for half in range(HALVES):
        own_pick[half].wait()
        for copy in stage2[half * len(flips) : (half + 1) * len(flips)]:
            copy.wait_recv()
        chain_send(0, half, False)

    panel_x, panel_y, panel_xy = panel_of(*X), panel_of(*Y), panel_of(1, 1, 0)
    from_xy = {}
    steps = 0
    for i in range(CHUNKS):
        cx, cy = order_x[i], order_y[i]
        from_x[cx].wait_recv()
        if i < CHUNKS // 2:
            from_xy[cx] = forward(panel_x, Y, cx)
        from_sib.append(forward(panel_x, SIB, cx))
        from_y[cy].wait_recv()
        if i < CHUNKS // 2:
            from_xy[cy] = forward(panel_y, X, cy)
        from_sib.append(forward(panel_y, SIB, cy))
        if i % 2 == 1 and steps < teams - 1:
            chain_step(steps)
            steps += 1
    for c in order_x:
        c = order_x[c // 2] if c % 2 == 0 else order_y[c // 2]
        from_xy[c].wait_recv()
        from_sib.append(forward(panel_xy, SIB, c))
    while steps < teams - 1:
        chain_step(steps)
        steps += 1
    for copy in from_sib:
        copy.wait_recv()
    for copy in sent:
        copy.wait_send()
    for k in range(teams - 1):
        for half in range(HALVES):
            chain_send(k, half, True)
    own_hidden.wait()


def gather(columns, hidden, out_grad, panels):
    teams = lax.axis_size("team")
    panel_rows, units = hidden.shape
    picks = columns.shape[1]
    copies = (3 * (teams - 1) + panels - 1) * HALVES + 7 * CHUNKS
    half_rows = panel_rows // teams // HALVES
    hbm = pl.BlockSpec(memory_space=pl.ANY)
    return pl.pallas_call(
        gather_kernel,
        out_shape=(
            jax.ShapeDtypeStruct((panels, panel_rows, units), hidden.dtype),
            jax.ShapeDtypeStruct((panels, panel_rows, picks * BS), out_grad.dtype),
        ),
        in_specs=[pl.BlockSpec(memory_space=pltpu.SMEM), hbm, hbm],
        out_specs=(hbm, hbm),
        scratch_shapes=[
            pltpu.VMEM((panel_rows // teams, teams * out_grad.shape[1]), out_grad.dtype),
            pltpu.VMEM(
                (HALVES, teams * out_grad.shape[1] // BS, half_rows, BS), out_grad.dtype
            ),
            pltpu.VMEM((HALVES, panels, half_rows, picks * BS), out_grad.dtype),
            pltpu.SemaphoreType.DMA((copies,)),
            pltpu.SemaphoreType.DMA((copies,)),
            pltpu.SemaphoreType.DMA((1 + 2 * HALVES,)),
        ],
        compiler_params=pltpu.CompilerParams(collective_id=0, has_side_effects=True),
    )(columns, hidden, out_grad)


def block_kernel(rows_ref, alive_ref, h_ref, g_ref, out_ref, ssq_ref):
    j = pl.program_id(0)
    per_column = out_ref.shape[0]
    scale = alive_ref[j].astype(jnp.float32)
    g_t = g_ref[...].T
    for k in range(0, per_column, 2):
        pair = []
        for i in (k, k + 1):
            r = rows_ref[j * per_column + i]
            pair.append(h_ref[:, pl.ds(pl.multiple_of(r * BS, BS), BS)])
        both = jnp.dot(
            g_t, jnp.concatenate(pair, axis=1), preferred_element_type=jnp.float32
        )
        for i in range(2):
            block = both[:, i * BS : (i + 1) * BS].T * scale
            out_ref[k + i] = block
            ssq_ref[0, k + i, :] = jnp.sum(block * block, axis=0)


def blocks(rows, alive, hidden, grad):
    picks = alive.shape[0]
    per_column = rows.shape[0] // picks
    tokens, units = hidden.shape
    return pl.pallas_call(
        block_kernel,
        out_shape=(
            jax.ShapeDtypeStruct((picks * per_column, BS, BS), jnp.float32),
            jax.ShapeDtypeStruct((picks, per_column, BS), jnp.float32),
        ),
        grid_spec=pltpu.PrefetchScalarGridSpec(
            num_scalar_prefetch=2,
            grid=(picks,),
            in_specs=[
                pl.BlockSpec(
                    (tokens, units), lambda j, *_: (0, 0), pipeline_mode=pl.Buffered(1)
                ),
                pl.BlockSpec((tokens, BS), lambda j, *_: (0, j)),
            ],
            out_specs=(
                pl.BlockSpec((per_column, BS, BS), lambda j, *_: (j, 0, 0)),
                pl.BlockSpec((1, per_column, BS), lambda j, *_: (j, 0, 0)),
            ),
        ),
        compiler_params=pltpu.CompilerParams(dimension_semantics=("arbitrary",)),
    )(rows, alive, hidden, grad)


def in_plane(hidden, out_grad, act_rows, col_owner):
    owners_count, cores = lax.axis_size("blk"), lax.axis_size("dp")
    column_blocks = col_owner.shape[0]
    capacity = min(3 * column_blocks // (2 * owners_count), 3 * column_blocks // 4)
    owned_all, alive_all = owner_tables(col_owner, owners_count, capacity)
    panels = owners_count * cores
    picks = capacity // cores
    columns = owned_all.reshape(panels, picks)
    mine = lax.axis_index("blk") * cores + lax.axis_index("dp")
    columns_mine = lax.dynamic_index_in_dim(columns, mine, 0, keepdims=False)
    alive_mine = lax.dynamic_index_in_dim(
        alive_all.reshape(panels, picks), mine, 0, keepdims=False
    ).astype(jnp.int32)
    rows = jnp.take(act_rows[0], columns_mine, axis=0).reshape(-1)
    hidden_all, grad_mine = gather(columns, hidden, out_grad, panels)
    tokens = panels * hidden.shape[0]
    gradients, ssq = blocks(
        rows,
        alive_mine,
        hidden_all.reshape(tokens, hidden.shape[1]),
        grad_mine.reshape(tokens, picks * BS),
    )
    mean = jnp.sum(ssq, axis=2).reshape(-1) * (1.0 / (BS * BS))
    scores = jnp.sqrt(mean + epsilon)
    return (gradients[None, None], scores[None, None])


def on_device(hidden, out_grad, act_rows, col_owner):
    owners_count = lax.axis_size("blk")
    owner_index = lax.axis_index("blk")
    column_blocks = col_owner.shape[0]
    capacity = min(3 * column_blocks // (2 * owners_count), 3 * column_blocks // 4)
    per_column = act_rows.shape[2]
    owned_all, alive_all = owner_tables(col_owner, owners_count, capacity)
    owned_mine = lax.dynamic_index_in_dim(owned_all, owner_index, 0, keepdims=False)
    alive_mine = lax.dynamic_index_in_dim(alive_all, owner_index, 0, keepdims=False)
    block_rows = jnp.take(act_rows[0], owned_mine, axis=0).reshape(-1)
    grad_full = lax.all_gather(out_grad, "team", axis=1, tiled=True)
    grad_mask = alive_mine.astype(jnp.bfloat16)[None, :, None]
    hidden_piece = lax.all_gather(hidden, "blk", axis=0, tiled=True)
    grad_piece = lax.all_gather(grad_full, "blk", axis=0, tiled=True)
    count_rows = grad_piece.shape[0]
    picked_grad = (
        jnp.take(grad_piece.reshape(count_rows, column_blocks, BS), owned_mine, axis=1) * grad_mask
    )
    hidden_blocks = hidden_piece.reshape(count_rows, -1, BS)
    picked_hidden = jnp.take(hidden_blocks, block_rows, axis=1).reshape(
        count_rows, capacity, per_column, BS
    )
    partial_value = jnp.einsum(
        "ncki,ncj->ckij", picked_hidden, picked_grad, preferred_element_type=jnp.float32
    )
    partial_value = partial_value.reshape(capacity * per_column, BS, BS)
    gradients = lax.psum_scatter(partial_value, "dp", scatter_dimension=0, tiled=True)
    scores = jnp.sqrt(jnp.mean(gradients * gradients, axis=(1, 2)) + epsilon)
    return (gradients[None, None], scores[None, None])


def solution(mesh):
    in_specs = (P(("blk", "dp"), "team"), P(("blk", "dp"), "team"), P("team", None, None), P())
    out_specs = (P("team", "blk", "dp", None, None), P("team", "blk", "dp"))
    square = mesh.shape["blk"] == 4 and mesh.shape["dp"] == 2
    return jax.shard_map(
        in_plane if square else on_device,
        mesh=mesh,
        in_specs=in_specs,
        out_specs=out_specs,
        check_vma=False,
    )
```

```python
import functools

import jax
import jax.numpy as jnp
from jax import lax
from jax.experimental import pallas as pl
from jax.experimental.pallas import tpu as pltpu
from jax.sharding import PartitionSpec as P

BS = 128
MESH = pl.DeviceIdType.MESH
CHUNKS = 4
HALVES = 2


epsilon = 1e-06


def owner_tables(col_owner, owners_count, capacity):
    column_blocks = col_owner.shape[0]
    owners = jnp.arange(owners_count, dtype=jnp.int32)
    onehot = (col_owner[:, None] == owners[None, :]).astype(jnp.int32)
    column_rank = jnp.sum((jnp.cumsum(onehot, axis=0) - onehot) * onehot, axis=1)
    slot_ids = jnp.arange(capacity, dtype=jnp.int32)
    matches = (col_owner[None, None, :] == owners[:, None, None]) & (
        column_rank[None, None, :] == slot_ids[None, :, None]
    )
    owned_all = jnp.sum(
        matches.astype(jnp.int32) * jnp.arange(column_blocks, dtype=jnp.int32)[None, None, :],
        axis=2,
    )
    return owned_all, jnp.any(matches, axis=2)


def gather_kernel(
    cols_ref, hid_ref, grad_ref, hfull, gfull, gz, gcol, snd, send_sem, recv_sem, local_sem
):
    teams = lax.axis_size("team")
    b, t, d = lax.axis_index("blk"), lax.axis_index("team"), lax.axis_index("dp")
    y, x = b // 2, b % 2
    panels, panel_rows, _ = hfull.shape
    part_rows = panel_rows // teams
    part_cols = grad_ref.shape[1]
    picks = cols_ref.shape[1]
    chunk = panel_rows // CHUNKS

    def plane(sy, sx, sd):
        oy = 1 - y if sy else y
        ox = 1 - x if sx else x
        return oy * 2 + ox, (1 - d if sd else d)

    def panel_of(sy, sx, sd):
        ob, od = plane(sy, sx, sd)
        return ob * 2 + od

    def device(sy, sx, sd):
        ob, od = plane(sy, sx, sd)
        return (ob, t, od)

    mine = panel_of(0, 0, 0)
    flips = [(sy, sx, sd) for sy in (0, 1) for sx in (0, 1) for sd in (0, 1)][1:]

    barrier = pltpu.get_barrier_semaphore()
    for flip in flips:
        pl.semaphore_signal(barrier, inc=1, device_id=device(*flip), device_id_type=MESH)
    for s in range(1, teams):
        pl.semaphore_signal(
            barrier, inc=1, device_id=(b, (t + s) % teams, d), device_id_type=MESH
        )
    pl.semaphore_wait(barrier, len(flips) + teams - 1)

    counter = [0]

    def remote(src, dst, target, slot=None):
        if slot is None:
            slot = counter[0]
            counter[0] += 1
        return pltpu.make_async_remote_copy(
            src_ref=src,
            dst_ref=dst,
            send_sem=send_sem.at[slot],
            recv_sem=recv_sem.at[slot],
            device_id=target,
            device_id_type=MESH,
        )

    sent = []

    def rows_of(c):
        return pl.ds(c * chunk, chunk)

    def send_own(flip, c):
        copy = remote(hid_ref.at[rows_of(c)], hfull.at[mine, rows_of(c)], device(*flip))
        copy.start()
        sent.append(copy)
        return copy

    def forward(panel, flip, c):
        piece = hfull.at[panel, rows_of(c)]
        copy = remote(piece, piece, device(*flip))
        copy.start()
        sent.append(copy)
        return copy

    half_rows = part_rows // HALVES

    def part(k, half):
        return pl.ds(k * part_rows + half * half_rows, half_rows)

    def held(half):
        return pl.ds(half * half_rows, half_rows)

    def quarter(k):
        return pl.ds(k * part_cols, part_cols)

    own_grad, stage1 = [], []
    for half in range(HALVES):
        for s in range(1, teams):
            target = (t + s) % teams
            copy = remote(
                grad_ref.at[part(target, half)],
                gz.at[held(half), quarter(t)],
                (b, target, d),
            )
            copy.start()
            stage1.append(copy)
            sent.append(copy)
        own_grad.append(
            pltpu.make_async_copy(
                grad_ref.at[part(t, half)],
                gz.at[held(half), quarter(t)],
                local_sem.at[1 + half],
            )
        )
        own_grad[half].start()

    order_x = list(range(CHUNKS))
    order_y = order_x[CHUNKS // 2 :] + order_x[: CHUNKS // 2]
    X, Y, SIB = (0, 1, 0), (1, 0, 0), (0, 0, 1)
    from_x, from_y, from_sib = {}, {}, []
    from_x[order_x[0]] = send_own(X, order_x[0])
    from_y[order_y[0]] = send_own(Y, order_y[0])
    own_hidden = pltpu.make_async_copy(hid_ref, hfull.at[mine], local_sem.at[0])
    own_hidden.start()

    own_pick, stage2 = [], []
    for half in range(HALVES):
        own_grad[half].wait()
        for copy in stage1[half * (teams - 1) : (half + 1) * (teams - 1)]:
            copy.wait_recv()
        rows = slice(half * half_rows, (half + 1) * half_rows)
        for c in range(gcol.shape[1]):
            gcol[half, c] = gz[rows, c * BS : (c + 1) * BS]

        def pick(p, carry):
            for j in range(picks):
                snd[half, p, :, j * BS : (j + 1) * BS] = gcol[half, cols_ref[p, j]]
            return carry

        lax.fori_loop(0, panels, pick, 0)
        landing = gfull.at[mine, part(t, half)]
        for flip in flips:
            copy = remote(snd.at[half, panel_of(*flip)], landing, device(*flip))
            copy.start()
            stage2.append(copy)
            sent.append(copy)
        own_pick.append(
            pltpu.make_async_copy(
                snd.at[half, mine], landing, local_sem.at[1 + HALVES + half]
            )
        )
        own_pick[half].start()

    for i in range(1, CHUNKS):
        from_x[order_x[i]] = send_own(X, order_x[i])
        from_y[order_y[i]] = send_own(Y, order_y[i])
    for c in range(CHUNKS):
        from_sib.append(send_own(SIB, c))

    chain_base = counter[0]
    counter[0] += 2 * (teams - 1) * HALVES

    def chain(up, k, shard, target, half):
        piece = gfull.at[:, part(shard, half)]
        step = k if up else teams - 1 + k
        return remote(piece, piece, (b, target, d), chain_base + step * HALVES + half)

    def chain_send(k, half, wait):
        @pl.when((t < teams - 1) & (t - k >= 0))
        def _():
            copy = chain(True, k, t - k, t + 1, half)
            copy.wait_send() if wait else copy.start()

        @pl.when((t > 0) & (t + k < teams))
        def _():
            copy = chain(False, k, t + k, t - 1, half)
            copy.wait_send() if wait else copy.start()

    def chain_recv(k, half):
        @pl.when(t - 1 - k >= 0)
        def _():
            chain(True, k, t - 1 - k, t - 1, half).wait_recv()

        @pl.when(t + 1 + k < teams)
        def _():
            chain(False, k, t + 1 + k, t + 1, half).wait_recv()

    def chain_step(k):
        for half in range(HALVES):
            chain_recv(k, half)
            if k < teams - 2:
                chain_send(k + 1, half, False)

    for half in range(HALVES):
        own_pick[half].wait()
        for copy in stage2[half * len(flips) : (half + 1) * len(flips)]:
            copy.wait_recv()
        chain_send(0, half, False)

    panel_x, panel_y, panel_xy = panel_of(*X), panel_of(*Y), panel_of(1, 1, 0)
    from_xy = {}
    steps = 0
    for i in range(CHUNKS):
        cx, cy = order_x[i], order_y[i]
        from_x[cx].wait_recv()
        if i < CHUNKS // 2:
            from_xy[cx] = forward(panel_x, Y, cx)
        from_sib.append(forward(panel_x, SIB, cx))
        from_y[cy].wait_recv()
        if i < CHUNKS // 2:
            from_xy[cy] = forward(panel_y, X, cy)
        from_sib.append(forward(panel_y, SIB, cy))
        if i % 2 == 1 and steps < teams - 1:
            chain_step(steps)
            steps += 1
    for c in order_x:
        c = order_x[c // 2] if c % 2 == 0 else order_y[c // 2]
        from_xy[c].wait_recv()
        from_sib.append(forward(panel_xy, SIB, c))
    while steps < teams - 1:
        chain_step(steps)
        steps += 1
    for copy in from_sib:
        copy.wait_recv()
    for copy in sent:
        copy.wait_send()
    for k in range(teams - 1):
        for half in range(HALVES):
            chain_send(k, half, True)
    own_hidden.wait()


def gather(columns, hidden, out_grad, panels):
    teams = lax.axis_size("team")
    panel_rows, units = hidden.shape
    picks = columns.shape[1]
    copies = (3 * (teams - 1) + panels - 1) * HALVES + 7 * CHUNKS
    half_rows = panel_rows // teams // HALVES
    hbm = pl.BlockSpec(memory_space=pl.ANY)
    return pl.pallas_call(
        gather_kernel,
        out_shape=(
            jax.ShapeDtypeStruct((panels, panel_rows, units), hidden.dtype),
            jax.ShapeDtypeStruct((panels, panel_rows, picks * BS), out_grad.dtype),
        ),
        in_specs=[pl.BlockSpec(memory_space=pltpu.SMEM), hbm, hbm],
        out_specs=(hbm, hbm),
        scratch_shapes=[
            pltpu.VMEM((panel_rows // teams, teams * out_grad.shape[1]), out_grad.dtype),
            pltpu.VMEM(
                (HALVES, teams * out_grad.shape[1] // BS, half_rows, BS), out_grad.dtype
            ),
            pltpu.VMEM((HALVES, panels, half_rows, picks * BS), out_grad.dtype),
            pltpu.SemaphoreType.DMA((copies,)),
            pltpu.SemaphoreType.DMA((copies,)),
            pltpu.SemaphoreType.DMA((1 + 2 * HALVES,)),
        ],
        compiler_params=pltpu.CompilerParams(collective_id=0, has_side_effects=True),
    )(columns, hidden, out_grad)


def block_kernel(rows_ref, alive_ref, h_ref, g_ref, out_ref, ssq_ref):
    j = pl.program_id(0)
    per_column = out_ref.shape[0]
    scale = alive_ref[j].astype(jnp.float32)
    g = g_ref[...]
    for k in range(0, per_column, 4):
        group = []
        for i in range(k, k + 4):
            r = rows_ref[j * per_column + i]
            group.append(h_ref[:, pl.ds(pl.multiple_of(r * BS, BS), BS)])
        product = lax.dot_general(
            jnp.concatenate(group, axis=1),
            g,
            (((0,), (0,)), ((), ())),
            preferred_element_type=jnp.float32,
        )
        block = product.reshape(4, BS, BS) * scale
        out_ref[k : k + 4] = block
        ssq_ref[0, k : k + 4, :] = jnp.sum(block * block, axis=1)


def blocks(rows, alive, hidden, grad):
    picks = alive.shape[0]
    per_column = rows.shape[0] // picks
    tokens, units = hidden.shape
    return pl.pallas_call(
        block_kernel,
        out_shape=(
            jax.ShapeDtypeStruct((picks * per_column, BS, BS), jnp.float32),
            jax.ShapeDtypeStruct((picks, per_column, BS), jnp.float32),
        ),
        grid_spec=pltpu.PrefetchScalarGridSpec(
            num_scalar_prefetch=2,
            grid=(picks,),
            in_specs=[
                pl.BlockSpec(
                    (tokens, units), lambda j, *_: (0, 0), pipeline_mode=pl.Buffered(1)
                ),
                pl.BlockSpec((tokens, BS), lambda j, *_: (0, j)),
            ],
            out_specs=(
                pl.BlockSpec((per_column, BS, BS), lambda j, *_: (j, 0, 0)),
                pl.BlockSpec((1, per_column, BS), lambda j, *_: (j, 0, 0)),
            ),
        ),
        compiler_params=pltpu.CompilerParams(dimension_semantics=("arbitrary",)),
    )(rows, alive, hidden, grad)


def in_plane(hidden, out_grad, act_rows, col_owner):
    owners_count, cores = lax.axis_size("blk"), lax.axis_size("dp")
    column_blocks = col_owner.shape[0]
    capacity = min(3 * column_blocks // (2 * owners_count), 3 * column_blocks // 4)
    owned_all, alive_all = owner_tables(col_owner, owners_count, capacity)
    panels = owners_count * cores
    picks = capacity // cores
    columns = owned_all.reshape(panels, picks)
    mine = lax.axis_index("blk") * cores + lax.axis_index("dp")
    columns_mine = lax.dynamic_index_in_dim(columns, mine, 0, keepdims=False)
    alive_mine = lax.dynamic_index_in_dim(
        alive_all.reshape(panels, picks), mine, 0, keepdims=False
    ).astype(jnp.int32)
    rows = jnp.take(act_rows[0], columns_mine, axis=0).reshape(-1)
    hidden_all, grad_mine = gather(columns, hidden, out_grad, panels)
    tokens = panels * hidden.shape[0]
    gradients, ssq = blocks(
        rows,
        alive_mine,
        hidden_all.reshape(tokens, hidden.shape[1]),
        grad_mine.reshape(tokens, picks * BS),
    )
    mean = jnp.sum(ssq, axis=2).reshape(-1) * (1.0 / (BS * BS))
    scores = jnp.sqrt(mean + epsilon)
    return (gradients[None, None], scores[None, None])


def on_device(hidden, out_grad, act_rows, col_owner):
    owners_count = lax.axis_size("blk")
    owner_index = lax.axis_index("blk")
    column_blocks = col_owner.shape[0]
    capacity = min(3 * column_blocks // (2 * owners_count), 3 * column_blocks // 4)
    per_column = act_rows.shape[2]
    owned_all, alive_all = owner_tables(col_owner, owners_count, capacity)
    owned_mine = lax.dynamic_index_in_dim(owned_all, owner_index, 0, keepdims=False)
    alive_mine = lax.dynamic_index_in_dim(alive_all, owner_index, 0, keepdims=False)
    block_rows = jnp.take(act_rows[0], owned_mine, axis=0).reshape(-1)
    grad_full = lax.all_gather(out_grad, "team", axis=1, tiled=True)
    grad_mask = alive_mine.astype(jnp.bfloat16)[None, :, None]
    hidden_piece = lax.all_gather(hidden, "blk", axis=0, tiled=True)
    grad_piece = lax.all_gather(grad_full, "blk", axis=0, tiled=True)
    count_rows = grad_piece.shape[0]
    picked_grad = (
        jnp.take(grad_piece.reshape(count_rows, column_blocks, BS), owned_mine, axis=1) * grad_mask
    )
    hidden_blocks = hidden_piece.reshape(count_rows, -1, BS)
    picked_hidden = jnp.take(hidden_blocks, block_rows, axis=1).reshape(
        count_rows, capacity, per_column, BS
    )
    partial_value = jnp.einsum(
        "ncki,ncj->ckij", picked_hidden, picked_grad, preferred_element_type=jnp.float32
    )
    partial_value = partial_value.reshape(capacity * per_column, BS, BS)
    gradients = lax.psum_scatter(partial_value, "dp", scatter_dimension=0, tiled=True)
    scores = jnp.sqrt(jnp.mean(gradients * gradients, axis=(1, 2)) + epsilon)
    return (gradients[None, None], scores[None, None])


def solution(mesh):
    in_specs = (P(("blk", "dp"), "team"), P(("blk", "dp"), "team"), P("team", None, None), P())
    out_specs = (P("team", "blk", "dp", None, None), P("team", "blk", "dp"))
    square = mesh.shape["blk"] == 4 and mesh.shape["dp"] == 2
    return jax.shard_map(
        in_plane if square else on_device,
        mesh=mesh,
        in_specs=in_specs,
        out_specs=out_specs,
        check_vma=False,
    )
```
